256 devices in a mesh: basis: 8 (over z_lo, core), fit: 32 (over z_hi, x, y).
Axes of the slice: x: 4, y: 4, z: 8 (z_hi: 2, z_lo: 4; z = z_hi * 4 + z_lo), core: 2. Of those that a mesh axis runs over, the one named last changes fastest.
Arguments:
- integrals: bfloat16 [1024, 512, 1024], P('basis', 'fit'), may hold values from -6 to 6
- pair_mask: int32 [64, 64], replicated, may hold values 0 or 1
- row_blocks: int32 [64], replicated, may hold values from 0 to 63, each once
- occ_coef: bfloat16 [1024, 64], P('basis'), may hold values from -0.25 to 0.25
- vir_coef: bfloat16 [1024, 32768], P(None, 'fit'), may hold values from -0.1875 to 0.1875
Outputs:
- transformed: bfloat16 [512, 64, 32768], P(None, 'basis', 'fit')
The draws below stay inside these ranges and needn't reach their ends.
Inputs may be any that keep to these rules, and one draw needn't show every extreme that they name: `row_blocks`: each of the 64 atom blocks appears exactly once. `pair_mask`: 1 marks a significant pair of atom blocks.
All inputs are finite; a program needn't handle non-finite values.
Results may differ from the reference program's by a relative error of at most 0.0049.
Values may be sent and summed in bfloat16 or wider, within the bound.
A program may use at most 128 MiB of HBM per device.

```python
import jax
import jax.numpy as jnp
from jax import lax

BLK = 16
NU = 1024
FIT_DEV = 16
NOCC = 64
NMU = 1024
NP = 512
NVIRW = 32768
NMB = 64
NNB = 64
N_FIT = 32


def with_ends(values, stream_key, least, top_value):
    place = [jax.random.randint(jax.random.fold_in(stream_key, axis), (), 0, length) for axis, length in enumerate(values.shape)]
    longest = values.shape.index(max(values.shape))
    beside = place[:longest] + [(place[longest] + 1) % values.shape[longest]] + place[longest + 1:]
    return values.at[tuple(place)].set(least).at[tuple(beside)].set(top_value)


def raised(values, own_key, source, target, blocks, factor):
    owner, partner = [(jnp.arange(values.shape[position]) // (values.shape[position] // blocks)).reshape([-1 if axis == position else 1 for axis in range(values.ndim)]) for position in (source, target)]
    chosen = jax.random.permutation(own_key, blocks)[partner]
    strong = (owner == chosen) | (owner == (partner + blocks // 2) % blocks)
    return jnp.where(strong, factor * values, values)


def shard_levels(rng, shape, cuts, low, high):
    def one(axis_at, shards_of):
        heights = jax.random.uniform(jax.random.fold_in(jax.random.fold_in(rng, 6), axis_at), (shards_of,), jnp.float32, low / len(cuts), high / len(cuts))
        return jnp.repeat(jnp.exp(heights), shape[axis_at] // shards_of).reshape((-1,) + (1,) * (len(shape) - axis_at - 1))

    loudness = one(*cuts[0])
    for cut in cuts[1:]:
        loudness = loudness * one(*cut)
    return loudness


def bell_draw(key, shape, spread, bound, shards=(), kind=jnp.bfloat16):
    values = spread * jax.random.normal(key, shape, jnp.float32)
    if shards:
        values = values * shard_levels(key, shape, shards, -0.22, 0.18)
    return jnp.clip(values, -bound, bound).astype(kind)


def heavy_noise(stream_key, shape, deviation, bound, split, heavy, kind=jnp.bfloat16):
    drawn = deviation * jax.random.normal(stream_key, shape, jnp.float32)
    if split:
        drawn = drawn * shard_levels(stream_key, shape, split, -0.22, 0.18)
    return jnp.clip(raised(drawn, jax.random.fold_in(stream_key, 3), *heavy), -bound, bound).astype(kind)


def setup_inputs(seed: int = 0) -> dict:
    streams_of = jax.random.split(jax.random.key(seed), 6)
    integrals = bell_draw(streams_of[0], (NMU, NP, NU), 1.0, 6.0, ((0, 8), (1, 32)))
    pair_mask = with_ends((jax.random.randint(streams_of[1], (NMB, NNB), 0, 3) < 2).astype(jnp.int32), jax.random.fold_in(streams_of[1], 1), 0, 1)
    row_blocks = jax.random.permutation(streams_of[2], NMB).astype(jnp.int32)
    occ_coef = heavy_noise(streams_of[3], (NMU, NOCC), NMU ** -0.5, 0.25, ((0, 8),), (0, 1, 8, 2.0))
    vir_coef = bell_draw(streams_of[4], (NU, NVIRW), NU ** -0.5, 0.1875, ((1, 32),))
    return dict(integrals=integrals, pair_mask=pair_mask, row_blocks=row_blocks, occ_coef=occ_coef, vir_coef=vir_coef)


def reference(integrals, pair_mask, row_blocks, occ_coef, vir_coef):
    blocks = occ_coef.reshape(NMB, BLK, NOCC)
    occ_rows = jnp.take(blocks, row_blocks.astype(jnp.int32), axis=0)
    mask_rows = jnp.take(pair_mask, row_blocks.astype(jnp.int32), axis=0)
    mask_full = jnp.repeat(mask_rows, BLK, axis=1).astype(jnp.bfloat16)
    x_blocks = integrals.reshape(NMB, BLK, NP, NU)

    def add_block(total, item):
        x_block, c_block, m_block = item
        masked = (x_block * m_block[None, None, :]).reshape(BLK, NP * NU)
        term = lax.dot_general(c_block, masked, (((0,), (0,)), ((), ())), preferred_element_type=jnp.float32)
        return total + term, None

    start = jnp.zeros((NOCC, NP * NU), jnp.float32)
    total, _ = lax.scan(add_block, start, (x_blocks, occ_rows, mask_full))
    half = total.astype(jnp.bfloat16).reshape(NOCC, NP, NU)
    half = jnp.transpose(half, (1, 0, 2)).reshape(N_FIT, FIT_DEV * NOCC, NU)

    def project(group):
        return jnp.dot(group, vir_coef, preferred_element_type=jnp.float32).astype(jnp.bfloat16)

    result = lax.map(project, half)
    return result.reshape(NP, NOCC, NVIRW)
```

```python
import jax
import jax.numpy as jnp
from jax import lax
from jax.experimental import pallas as pl
from jax.experimental.pallas import tpu as pltpu
from jax.sharding import PartitionSpec as P

BLK = 16
NB = 8
NC = 8
N = 1024
HALF = N // 2
F32 = jnp.float32
BF16 = jnp.bfloat16

SIB, Z1, ZH = 0, 1, 4
RING = 5
KINDS = RING + 16
A_UP, A_DN, A_FUP, A_FDN, B_UP, B_DN, B_FUP, B_FDN = range(8)


def kernel(rb_ref, mask_ref, x_hbm, occ_hbm, vir_hbm, out_hbm,
           xv, occ_all, vir, t1, p32, zacc, sib_tx, sib_rx, z_tx, z_rx, g, obuf,
           x_sem, vir_sem, own_sem, out_sem, occ_send, occ_recv, send, recv):
    b = lax.axis_index("basis")
    f = lax.axis_index("fit")
    core, zl = b % 2, b // 2
    zh, x, y = f // 16, (f // 4) % 4, f % 4
    sib = zl * 2 + (1 - core)
    other = (f + 16) % 32
    xp, xm = (x + 1) % 4, (x + 3) % 4
    yp, ym = (y + 1) % 4, (y + 3) % 4
    f_x = (zh * 16 + xp * 4 + y, zh * 16 + xm * 4 + y)
    f_y = (zh * 16 + x * 4 + yp, zh * 16 + x * 4 + ym)

    def remote(src, dst, ssem, rsem, bb, ff):
        return pltpu.make_async_remote_copy(
            src_ref=src, dst_ref=dst, send_sem=ssem, recv_sem=rsem,
            device_id=(bb, ff), device_id_type=pl.DeviceIdType.MESH)

    x_copies = [pltpu.make_async_copy(x_hbm.at[pl.ds(r * 256, 256)], xv.at[pl.ds(r * 256, 256)], x_sem.at[r])
                for r in range(NB)]
    own_copy = pltpu.make_async_copy(occ_hbm, occ_all.at[b], own_sem)
    vir_copy = pltpu.make_async_copy(vir_hbm, vir, vir_sem)
    own_copy.start()
    for c in x_copies:
        c.start()
    vir_copy.start()

    barrier = pltpu.get_barrier_semaphore()
    partners = [((b + d) % NB, f) for d in range(1, NB)] + [(b, other)] + [(b, q) for q in f_x + f_y]
    for bb, ff in partners:
        pl.semaphore_signal(barrier, inc=1, device_id=(bb, ff), device_id_type=pl.DeviceIdType.MESH)
    pl.semaphore_wait(barrier, len(partners))

    def occ_copy(d):
        return remote(occ_hbm, occ_all.at[b], occ_send.at[d - 1], occ_recv.at[d - 1], (b + d) % NB, f)

    def occ_arrival(d):
        slot = occ_all.at[(b + NB - d) % NB]
        return remote(slot, slot, occ_send.at[d - 1], occ_recv.at[d - 1], (b + d) % NB, f)

    for d in range(1, NB):
        occ_copy(d).start()

    owned = [rb_ref[b * NB + r] for r in range(NB)]
    sub8 = lax.broadcasted_iota(jnp.int32, (NB, 64), 0)
    lane64 = lax.broadcasted_iota(jnp.int32, (NB, 64), 1)
    want = jnp.zeros((NB, 64), jnp.int32)
    for r in range(NB):
        want = jnp.where(sub8 == r, owned[r], want)
    pick = jnp.where(lane64 == want, 1.0, 0.0).astype(BF16)
    rows = jnp.dot(pick, mask_ref[...].astype(F32).astype(BF16), preferred_element_type=F32).astype(BF16)
    spread = jnp.where(
        lax.broadcasted_iota(jnp.int32, (64, N), 1) // BLK == lax.broadcasted_iota(jnp.int32, (64, N), 0),
        1.0, 0.0).astype(BF16)
    mask_cols = jnp.dot(rows, spread, preferred_element_type=F32)
    for r in range(NB):
        x_copies[r].wait()
        m = jnp.broadcast_to(mask_cols[r:r + 1, :], (16, N)).astype(BF16)
        for s in range(16):
            at = pl.ds(r * 256 + s * 16, 16)
            xv[at, :] = xv[at, :] * m

    lane_m = lax.broadcasted_iota(jnp.int32, (128, 128), 1)
    source = jnp.zeros((128, 128), jnp.int32)
    for r in range(NB):
        source = jnp.where(lane_m // BLK == r, owned[r] * BLK + lane_m % BLK, source)
    sub_m = lax.broadcasted_iota(jnp.int32, (128, 128), 0)
    own_copy.wait()
    for d in range(1, NB):
        occ_arrival(d).wait_recv()
    occ_sel = jnp.zeros((64, 128), F32)
    for d in range(NB):
        sel = jnp.where(source == sub_m + d * 128, 1.0, 0.0).astype(BF16)
        occ_sel = occ_sel + jnp.dot(occ_all[d], sel, preferred_element_type=F32)
    rep = jnp.where(
        lax.broadcasted_iota(jnp.int32, (128, 2048), 1) // 16 == lax.broadcasted_iota(jnp.int32, (128, 2048), 0),
        1.0, 0.0).astype(BF16)
    t1[...] = jnp.dot(occ_sel.astype(BF16), rep, preferred_element_type=F32)
    vir_copy.wait()

    def sib_copy(c):
        return remote(sib_tx.at[c], sib_rx.at[c], send.at[c, SIB], recv.at[c, SIB], sib, f)

    def z_copy(c, d):
        to = (zl + d) % 4
        return remote(z_tx.at[c, to], z_rx.at[c, d - 1], send.at[c, Z1 + d - 1], recv.at[c, Z1 + d - 1],
                      to * 2 + core, f)

    def zh_copy(c):
        here = g.at[zh, x, y, c]
        return remote(here, here, send.at[c, ZH], recv.at[c, ZH], b, other)

    def zh_arrival(c):
        here = g.at[1 - zh, x, y, c]
        return remote(here, here, send.at[c, ZH], recv.at[c, ZH], b, other)

    def block(k, pos, c):
        return g.at[zh, pos, y, c] if k == 0 else g.at[1 - zh, x, pos, c]

    def group(k, lo, n, pos, c):
        return g.at[zh, pl.ds(lo, n), pos, c] if k == 0 else g.at[1 - zh, pos, pl.ds(lo, n), c]

    def lane_half(ref, h):
        return ref.at[:, pl.ds(h * HALF, HALF)]

    ring1 = ((x, xp, xm, (x + 2) % 4, f_x), (y, yp, ym, (y + 2) % 4, f_y))
    ring2 = (ring1[1], ring1[0])

    def ring_copy(k, j, c, arrival):
        me, up, dn, opp, to = (ring1 if j < B_UP else ring2)[k]
        if j == A_UP:
            ref, dev = block(k, dn if arrival else me, c), to[0]
        elif j == A_DN:
            ref, dev = block(k, up if arrival else me, c), to[1]
        elif j == A_FUP:
            ref, dev = lane_half(block(k, opp if arrival else dn, c), 0), to[0]
        elif j == A_FDN:
            ref, dev = lane_half(block(k, opp if arrival else up, c), 1), to[1]
        elif j == B_UP:
            ref, dev = group(k, 0, 4, dn if arrival else me, c), to[0]
        elif j == B_DN:
            ref, dev = group(k, 0, 4, up if arrival else me, c), to[1]
        elif j == B_FUP:
            ref, dev = group(k, 0, 2, opp if arrival else dn, c), to[0]
        else:
            ref, dev = group(k, 2, 2, opp if arrival else up, c), to[1]
        s = RING + 8 * k + j
        return remote(ref, ref, send.at[c, s], recv.at[c, s], b, dev)

    def go(k, j, c):
        ring_copy(k, j, c, False).start()

    def arrived(k, j, c):
        ring_copy(k, j, c, True).wait_recv()

    col16 = lax.broadcasted_iota(jnp.int32, (8, 2, 8, 2048), 3) % 16
    row2 = lax.broadcasted_iota(jnp.int32, (8, 2, 8, 2048), 1)

    def stage0(c):
        w = jnp.where(col16 == 2 * c + row2, t1[...].reshape(8, 1, 8, 2048), 0.0)
        w = w.reshape(128, 2048).astype(BF16)
        part = jnp.dot(w, xv[...], preferred_element_type=F32)
        p32[...] = part.reshape(4, 2, 16, N)
        sib_tx[c] = p32[:, 1 - core].astype(BF16)
        sib_copy(c).start()
        zacc[c % 2] = p32[:, core]

    def stage1(c):
        sib_copy(c).wait_recv()
        total = zacc[c % 2] + sib_rx[c].astype(F32)
        zacc[c % 2] = total
        z_tx[c] = total.astype(BF16)
        for d in range(1, 4):
            z_copy(c, d).start()

    def stage2(c):
        half = zacc[c % 2, zl]
        for d in range(1, 4):
            z_copy(c, d).wait_recv()
            half = half + z_rx[c, d - 1].astype(F32)
        g[zh, x, y, c] = half.astype(BF16)
        zh_copy(c).start()
        go(0, A_UP, c)
        go(0, A_DN, c)

    def stage3(c):
        zh_arrival(c).wait_recv()
        go(1, A_UP, c)
        go(1, A_DN, c)
        arrived(0, A_UP, c)
        go(0, A_FUP, c)
        arrived(0, A_DN, c)
        go(0, A_FDN, c)

    def stage4(c):
        arrived(0, A_FUP, c)
        arrived(0, A_FDN, c)
        go(0, B_UP, c)
        go(0, B_DN, c)
        arrived(1, A_UP, c)
        go(1, A_FUP, c)
        arrived(1, A_DN, c)
        go(1, A_FDN, c)

    def stage5(c):
        arrived(1, A_FUP, c)
        arrived(1, A_FDN, c)
        go(1, B_UP, c)
        go(1, B_DN, c)
        arrived(0, B_UP, c)
        go(0, B_FUP, c)
        arrived(0, B_DN, c)
        go(0, B_FDN, c)

    def stage6(c):
        arrived(1, B_UP, c)
        go(1, B_FUP, c)
        arrived(1, B_DN, c)
        go(1, B_FDN, c)

    def stage7(c):
        arrived(0, B_FUP, c)
        arrived(0, B_FDN, c)
        arrived(1, B_FUP, c)
        arrived(1, B_FDN, c)

    def out_copy(c):
        return pltpu.make_async_copy(obuf.at[c], out_hbm.at[:, c], out_sem.at[c])

    def stage8(c):
        lhs = g[:, :, :, c].reshape(512, N)
        for q in range(2):
            cols = pl.ds(q * HALF, HALF)
            prod = jnp.dot(lhs, vir[:, cols], preferred_element_type=F32)
            obuf[c, :, :, cols] = prod.astype(BF16).reshape(32, 16, HALF)
        out_copy(c).start()

    stages = (stage7, stage6, stage5, stage4, stage3, stage2, stage1, stage0, stage8)
    lags = (7, 6, 5, 4, 3, 2, 1, 0, 7)

    def step(t, carry):
        for fn, lag in zip(stages, lags):
            c = t - lag

            @pl.when((c >= 0) & (c < NC))
            def _():
                fn(c)
        return carry

    lax.fori_loop(0, NC + 7, step, 0)

    def drain(c, carry):
        sib_copy(c).wait_send()
        for d in range(1, 4):
            z_copy(c, d).wait_send()
        zh_copy(c).wait_send()
        for k in range(2):
            for j in range(8):
                ring_copy(k, j, c, False).wait_send()
        out_copy(c).wait()
        return carry

    lax.fori_loop(0, NC, drain, 0)
    for d in range(1, NB):
        occ_copy(d).wait_send()


def shards(integrals, pair_mask, row_blocks, occ_coef, vir_coef):
    x2 = integrals.reshape(2048, N)
    hbm = pl.BlockSpec(memory_space=pl.ANY)
    out = pl.pallas_call(
        kernel,
        out_shape=jax.ShapeDtypeStruct((32, NC, 16, N), BF16),
        in_specs=[pl.BlockSpec(memory_space=pltpu.SMEM), pl.BlockSpec(memory_space=pltpu.VMEM), hbm, hbm, hbm],
        out_specs=hbm,
        scratch_shapes=[
            pltpu.VMEM((2048, N), BF16),
            pltpu.VMEM((NB, 64, 128), BF16),
            pltpu.VMEM((N, N), BF16),
            pltpu.VMEM((64, 2048), F32),
            pltpu.VMEM((4, 2, 16, N), F32),
            pltpu.VMEM((2, 4, 16, N), F32),
            pltpu.VMEM((NC, 4, 16, N), BF16),
            pltpu.VMEM((NC, 4, 16, N), BF16),
            pltpu.VMEM((NC, 4, 16, N), BF16),
            pltpu.VMEM((NC, 3, 16, N), BF16),
            pltpu.VMEM((2, 4, 4, NC, 16, N), BF16),
            pltpu.VMEM((NC, 32, 16, N), BF16),
            pltpu.SemaphoreType.DMA((NB,)),
            pltpu.SemaphoreType.DMA,
            pltpu.SemaphoreType.DMA,
            pltpu.SemaphoreType.DMA((NC,)),
            pltpu.SemaphoreType.DMA((NB - 1,)),
            pltpu.SemaphoreType.DMA((NB - 1,)),
            pltpu.SemaphoreType.DMA((NC, KINDS)),
            pltpu.SemaphoreType.DMA((NC, KINDS)),
        ],
        compiler_params=pltpu.CompilerParams(
            collective_id=0, has_side_effects=True, vmem_limit_bytes=56 * 2 ** 20),
        cost_estimate=pl.CostEstimate(flops=13 * 10 ** 9, bytes_accessed=15 * 2 ** 20, transcendentals=0),
    )(row_blocks, pair_mask, x2, occ_coef.T, vir_coef)
    return out.reshape(512, 8, N)


def solution(mesh):
    placed = (P("basis", "fit", None), P(), P(), P("basis", None), P(None, "fit"))
    return jax.shard_map(
        shards, mesh=mesh, in_specs=placed, out_specs=P(None, "basis", "fit"), check_vma=False
    )
```

```python
import jax
import jax.numpy as jnp
from jax import lax
from jax.experimental import pallas as pl
from jax.experimental.pallas import tpu as pltpu
from jax.sharding import PartitionSpec as P

BLK = 16
NB = 8
NP = 8
NC = 16
N = 1024
HALF = N // 2
QUART = N // 4
F32 = jnp.float32
BF16 = jnp.bfloat16

SIB, Z1, ZH = 0, 1, 4
RING = 5
KINDS = RING + 16
A_UP, A_DN, A_FUP, A_FDN, B_UP, B_DN, B_FUP, B_FDN = range(8)


def kernel(rb_hbm, mask_hbm, x_hbm, occ_hbm, vir_hbm, done_ref, last_ref, vir,
           rb_ref, mask_ref, xv, occ_all, t1, p32, zacc, sib_tx, sib_rx, z_tx, z_rx, g,
           rb_sem, mask_sem, x_sem, vir_sem, own_sem, occ_send, occ_recv, send, recv):
    b = lax.axis_index("basis")
    f = lax.axis_index("fit")
    core, zl = b % 2, b // 2
    zh, x, y = f // 16, (f // 4) % 4, f % 4
    sib = zl * 2 + (1 - core)
    other = (f + 16) % 32
    xp, xm = (x + 1) % 4, (x + 3) % 4
    yp, ym = (y + 1) % 4, (y + 3) % 4
    f_x = (zh * 16 + xp * 4 + y, zh * 16 + xm * 4 + y)
    f_y = (zh * 16 + x * 4 + yp, zh * 16 + x * 4 + ym)

    def remote(src, dst, ssem, rsem, bb, ff):
        return pltpu.make_async_remote_copy(
            src_ref=src, dst_ref=dst, send_sem=ssem, recv_sem=rsem,
            device_id=(bb, ff), device_id_type=pl.DeviceIdType.MESH)

    barrier = pltpu.get_barrier_semaphore()
    partners = [((b + d) % NB, f) for d in range(1, NB)] + [(b, other)] + [(b, q) for q in f_x + f_y]
    for bb, ff in partners:
        pl.semaphore_signal(barrier, inc=1, device_id=(bb, ff), device_id_type=pl.DeviceIdType.MESH)

    x_copies = [pltpu.make_async_copy(x_hbm.at[pl.ds(r * 256, 256)], xv.at[pl.ds(r * 256, 256)], x_sem.at[r])
                for r in range(NB)]
    own_copy = pltpu.make_async_copy(occ_hbm, occ_all.at[b], own_sem)
    vir_copy = pltpu.make_async_copy(vir_hbm, vir, vir_sem)
    rb_copy = pltpu.make_async_copy(rb_hbm, rb_ref, rb_sem)
    mask_copy = pltpu.make_async_copy(mask_hbm, mask_ref, mask_sem)
    own_copy.start()
    rb_copy.start()
    mask_copy.start()
    for c in x_copies:
        c.start()
    vir_copy.start()

    def occ_copy(d):
        return remote(occ_all.at[b], occ_all.at[b], occ_send.at[d - 1], occ_recv.at[d - 1], (b + d) % NB, f)

    def occ_arrival(d):
        slot = occ_all.at[(b + NB - d) % NB]
        return remote(slot, slot, occ_send.at[d - 1], occ_recv.at[d - 1], (b + d) % NB, f)

    own_copy.wait()
    pl.semaphore_wait(barrier, len(partners))
    for d in range(1, NB):
        occ_copy(d).start()
    rb_copy.wait()
    mask_copy.wait()

    owned = [rb_ref[b * NB + r] for r in range(NB)]
    sub8 = lax.broadcasted_iota(jnp.int32, (NB, 64), 0)
    lane64 = lax.broadcasted_iota(jnp.int32, (NB, 64), 1)
    want = jnp.zeros((NB, 64), jnp.int32)
    for r in range(NB):
        want = jnp.where(sub8 == r, owned[r], want)
    pick = jnp.where(lane64 == want, 1.0, 0.0).astype(BF16)
    rows = jnp.dot(pick, mask_ref[...].astype(F32).astype(BF16), preferred_element_type=F32).astype(BF16)
    spread = jnp.where(
        lax.broadcasted_iota(jnp.int32, (64, N), 1) // BLK == lax.broadcasted_iota(jnp.int32, (64, N), 0),
        1.0, 0.0).astype(BF16)
    mask_cols = jnp.dot(rows, spread, preferred_element_type=F32)
    for r in range(NB):
        x_copies[r].wait()
        m = jnp.broadcast_to(mask_cols[r:r + 1, :], (16, N)).astype(BF16)
        for s in range(16):
            at = pl.ds(r * 256 + s * 16, 16)
            xv[at, :] = xv[at, :] * m

    lane_m = lax.broadcasted_iota(jnp.int32, (128, 128), 1)
    source = jnp.zeros((128, 128), jnp.int32)
    for r in range(NB):
        source = jnp.where(lane_m // BLK == r, owned[r] * BLK + lane_m % BLK, source)
    sub_m = lax.broadcasted_iota(jnp.int32, (128, 128), 0)
    for d in range(1, NB):
        occ_arrival(d).wait_recv()
    occ_sel = jnp.zeros((64, 128), F32)
    for d in range(NB):
        sel = jnp.where(source == sub_m + d * 128, 1.0, 0.0).astype(BF16)
        occ_sel = occ_sel + jnp.dot(occ_all[d], sel, preferred_element_type=F32)
    rep = jnp.where(
        lax.broadcasted_iota(jnp.int32, (128, 2048), 1) // 16 == lax.broadcasted_iota(jnp.int32, (128, 2048), 0),
        1.0, 0.0).astype(BF16)
    t1[...] = jnp.dot(occ_sel.astype(BF16), rep, preferred_element_type=F32)
    vir_copy.wait()

    def sib_copy(c):
        return remote(sib_tx.at[c], sib_rx.at[c], send.at[c, SIB], recv.at[c, SIB], sib, f)

    def z_copy(c, d):
        to = (zl + d) % 4
        return remote(z_tx.at[c, to], z_rx.at[c, d - 1], send.at[c, Z1 + d - 1], recv.at[c, Z1 + d - 1],
                      to * 2 + core, f)

    def zh_copy(c):
        here = g.at[zh, x, y, c // 2, c % 2]
        return remote(here, here, send.at[c, ZH], recv.at[c, ZH], b, other)

    def zh_arrival(c):
        here = g.at[1 - zh, x, y, c // 2, c % 2]
        return remote(here, here, send.at[c, ZH], recv.at[c, ZH], b, other)

    def block(k, pos, c):
        return g.at[zh, pos, y, c // 2, c % 2] if k == 0 else g.at[1 - zh, x, pos, c // 2, c % 2]

    def group(k, lo, n, pos, c):
        if k == 0:
            return g.at[zh, pl.ds(lo, n), pos, c // 2, c % 2]
        return g.at[1 - zh, pos, pl.ds(lo, n), c // 2, c % 2]

    def lane_half(ref, h):
        return ref.at[:, pl.ds(h * QUART, QUART)]

    ring1 = ((x, xp, xm, (x + 2) % 4, f_x), (y, yp, ym, (y + 2) % 4, f_y))
    ring2 = (ring1[1], ring1[0])

    def ring_copy(k, j, c, arrival):
        me, up, dn, opp, to = (ring1 if j < B_UP else ring2)[k]
        if j == A_UP:
            ref, dev = block(k, dn if arrival else me, c), to[0]
        elif j == A_DN:
            ref, dev = block(k, up if arrival else me, c), to[1]
        elif j == A_FUP:
            ref, dev = lane_half(block(k, opp if arrival else dn, c), 0), to[0]
        elif j == A_FDN:
            ref, dev = lane_half(block(k, opp if arrival else up, c), 1), to[1]
        elif j == B_UP:
            ref, dev = group(k, 0, 4, dn if arrival else me, c), to[0]
        elif j == B_DN:
            ref, dev = group(k, 0, 4, up if arrival else me, c), to[1]
        elif j == B_FUP:
            ref, dev = group(k, 0, 2, opp if arrival else dn, c), to[0]
        else:
            ref, dev = group(k, 2, 2, opp if arrival else up, c), to[1]
        s = RING + 8 * k + j
        return remote(ref, ref, send.at[c, s], recv.at[c, s], b, dev)

    def go(k, j, c):
        ring_copy(k, j, c, False).start()

    def arrived(k, j, c):
        ring_copy(k, j, c, True).wait_recv()

    col16 = lax.broadcasted_iota(jnp.int32, (8, 2, 8, 2048), 3) % 16
    row2 = lax.broadcasted_iota(jnp.int32, (8, 2, 8, 2048), 1)

    def stage0(c):
        w = jnp.where(col16 == 2 * (c // 2) + row2, t1[...].reshape(8, 1, 8, 2048), 0.0)
        w = w.reshape(128, 2048).astype(BF16)
        cols = pl.ds(pl.multiple_of((c % 2) * HALF, HALF), HALF)
        part = jnp.dot(w, xv[:, cols], preferred_element_type=F32)
        p32[...] = part.reshape(4, 2, 16, HALF)
        sib_tx[c] = p32[:, 1 - core].astype(BF16)
        sib_copy(c).start()
        zacc[c] = p32[:, core]

    def stage1(c):
        sib_copy(c).wait_recv()
        total = zacc[c] + sib_rx[c].astype(F32)
        zacc[c] = total
        z_tx[c] = total.astype(BF16)
        for d in range(1, 4):
            z_copy(c, d).start()

    def stage2(c):
        half = zacc[c, zl]
        for d in range(1, 4):
            z_copy(c, d).wait_recv()
            half = half + z_rx[c, d - 1].astype(F32)
        g[zh, x, y, c // 2, c % 2] = half.astype(BF16)
        zh_copy(c).start()
        go(0, A_UP, c)
        go(0, A_DN, c)

    def stage3(c):
        zh_arrival(c).wait_recv()
        go(1, A_UP, c)
        go(1, A_DN, c)

    def stage8(c):
        q = c // 2

        @pl.when((c % 2 == 1) & (q < NP - 1))
        def _():
            low = g[:, :, :, q, 0].reshape(512, HALF)
            high = g[:, :, :, q, 1].reshape(512, HALF)
            prod = jnp.dot(low, vir[0:HALF, :], preferred_element_type=F32)
            prod = prod + jnp.dot(high, vir[HALF:N, :], preferred_element_type=F32)
            done_ref[q] = prod.astype(BF16).reshape(32, 16, N)

        @pl.when(c == NC - 1)
        def _():
            for h in range(2):
                last_ref[h] = g[:, :, :, NP - 1, h].reshape(512, HALF)

    def ring_a(k):
        def forward(c):
            arrived(k, A_UP, c)
            go(k, A_FUP, c)
            arrived(k, A_DN, c)
            go(k, A_FDN, c)

        def turn(c):
            arrived(k, A_FUP, c)
            arrived(k, A_FDN, c)
            go(k, B_UP, c)
            go(k, B_DN, c)
        return forward, turn

    def ring_b(k):
        def forward(c):
            arrived(k, B_UP, c)
            go(k, B_FUP, c)
            arrived(k, B_DN, c)
            go(k, B_FDN, c)

        def finish(c):
            arrived(k, B_FUP, c)
            arrived(k, B_FDN, c)
        return forward, finish

    (a20, a30), (a21, a31) = ring_a(0), ring_a(1)
    (a40, a50), (a41, a51) = ring_b(0), ring_b(1)
    schedule = ((a50, 11), (a51, 13), (a41, 11), (a40, 9), (a31, 9), (a30, 7), (a21, 7), (a20, 5), (stage3, 5), (stage2, 3), (stage1, 1), (stage0, 0), (stage8, 13))

    def step(t, carry):
        for fn, lag in schedule:
            c = t - lag

            @pl.when((c >= 0) & (c < NC))
            def _():
                fn(c)
        return carry

    lax.fori_loop(0, NC + max(lag for _, lag in schedule), step, 0)

    def drain(c, carry):
        sib_copy(c).wait_send()
        for d in range(1, 4):
            z_copy(c, d).wait_send()
        zh_copy(c).wait_send()
        for k in range(2):
            for j in range(8):
                ring_copy(k, j, c, False).wait_send()
        return carry

    lax.fori_loop(0, NC, drain, 0)
    for d in range(1, NB):
        occ_copy(d).wait_send()


def finish_kernel(done_ref, last_ref, vir_ref, out_hbm, tail, sem):
    copies = [pltpu.make_async_copy(done_ref.at[q], out_hbm.at[:, q], sem.at[q]) for q in range(NP - 1)]
    for copy in copies:
        copy.start()
    prod = jnp.dot(last_ref[0], vir_ref[0:HALF, :], preferred_element_type=F32)
    prod = prod + jnp.dot(last_ref[1], vir_ref[HALF:N, :], preferred_element_type=F32)
    tail[...] = prod.astype(BF16).reshape(32, 16, N)
    copy = pltpu.make_async_copy(tail, out_hbm.at[:, NP - 1], sem.at[NP - 1])
    copy.start()
    for copy in copies + [copy]:
        copy.wait()


def shards(integrals, pair_mask, row_blocks, occ_coef, vir_coef):
    x2 = integrals.reshape(2048, N)
    hbm = pl.BlockSpec(memory_space=pl.ANY)
    vmem = pl.BlockSpec(memory_space=pltpu.VMEM)
    done, last, vir = pl.pallas_call(
        kernel,
        out_shape=(pltpu.VMEM((NP - 1, 32, 16, N), BF16), pltpu.VMEM((2, 512, HALF), BF16),
                   pltpu.VMEM((N, N), BF16)),
        in_specs=[pl.BlockSpec(memory_space=pltpu.HBM)] * 5,
        out_specs=(vmem, vmem, vmem),
        scratch_shapes=[
            pltpu.SMEM((NB * NB,), jnp.int32),
            pltpu.VMEM((64, 64), jnp.int32),
            pltpu.VMEM((2048, N), BF16),
            pltpu.VMEM((NB, 64, 128), BF16),
            pltpu.VMEM((64, 2048), F32),
            pltpu.VMEM((4, 2, 16, HALF), F32),
            pltpu.VMEM((NC, 4, 16, HALF), F32),
            pltpu.VMEM((NC, 4, 16, HALF), BF16),
            pltpu.VMEM((NC, 4, 16, HALF), BF16),
            pltpu.VMEM((NC, 4, 16, HALF), BF16),
            pltpu.VMEM((NC, 3, 16, HALF), BF16),
            pltpu.VMEM((2, 4, 4, NP, 2, 16, HALF), BF16),
            pltpu.SemaphoreType.DMA,
            pltpu.SemaphoreType.DMA,
            pltpu.SemaphoreType.DMA((NB,)),
            pltpu.SemaphoreType.DMA,
            pltpu.SemaphoreType.DMA,
            pltpu.SemaphoreType.DMA((NB - 1,)),
            pltpu.SemaphoreType.DMA((NB - 1,)),
            pltpu.SemaphoreType.DMA((NC, KINDS)),
            pltpu.SemaphoreType.DMA((NC, KINDS)),
        ],
        compiler_params=pltpu.CompilerParams(
            collective_id=0, has_side_effects=True, vmem_limit_bytes=53900 * 1024),
        cost_estimate=pl.CostEstimate(flops=13 * 10 ** 9, bytes_accessed=15 * 2 ** 20, transcendentals=0),
    )(row_blocks, pair_mask, x2, occ_coef.T, vir_coef)
    out = pl.pallas_call(
        finish_kernel,
        out_shape=jax.ShapeDtypeStruct((32, NP, 16, N), BF16),
        in_specs=[vmem, vmem, vmem],
        out_specs=hbm,
        scratch_shapes=[pltpu.VMEM((32, 16, N), BF16), pltpu.SemaphoreType.DMA((NP,))],
        compiler_params=pltpu.CompilerParams(vmem_limit_bytes=12 * 2 ** 20),
    )(done, last, vir)
    return out.reshape(512, 8, N)


def solution(mesh):
    placed = (P("basis", "fit", None), P(), P(), P("basis", None), P(None, "fit"))
    return jax.shard_map(
        shards, mesh=mesh, in_specs=placed, out_specs=P(None, "basis", "fit"), check_vma=False
    )
```

```python
import jax
import jax.numpy as jnp
from jax import lax
from jax.experimental import pallas as pl
from jax.experimental.pallas import tpu as pltpu
from jax.sharding import PartitionSpec as P

BLK = 16
NB = 8
NP = 8
NC = 8
N = 1024
HALF = N // 2
QUART = N // 4
F32 = jnp.float32
BF16 = jnp.bfloat16

SIB, Z1, ZH = 0, 1, 4
RING = 5
PER_STREAM = 12
KINDS = RING + 4 * PER_STREAM
A_UP, A_DN, A_FUP, A_FDN, B0_UP, B0_DN, B1_UP, B1_DN, B2_UP, B2_DN, B_FUP, B_FDN = range(PER_STREAM)
ME, UP, DN, OPP = range(4)
FIRST = {A_UP: (ME, DN), A_DN: (ME, UP), A_FUP: (DN, OPP), A_FDN: (UP, OPP)}
SECOND = {B0_UP: (ME, DN, 0, 1), B0_DN: (ME, UP, 0, 1), B1_UP: (ME, DN, 1, 2), B1_DN: (ME, UP, 1, 2),
          B2_UP: (ME, DN, 3, 1), B2_DN: (ME, UP, 3, 1), B_FUP: (DN, OPP, 0, 2), B_FDN: (UP, OPP, 2, 2)}


def kernel(rb_hbm, mask_hbm, x_hbm, occ_hbm, vir_hbm, done_ref, last_ref, vir,
           rb_ref, mask_ref, xv, occ_all, t1, p32, zacc, sib_tx, sib_rx, z_tx, z_rx, g,
           rb_sem, mask_sem, x_sem, vir_sem, own_sem, occ_send, occ_recv, send, recv):
    b = lax.axis_index("basis")
    f = lax.axis_index("fit")
    core, zl = b % 2, b // 2
    zh, x, y = f // 16, (f // 4) % 4, f % 4
    sib = zl * 2 + (1 - core)
    other = (f + 16) % 32
    xp, xm = (x + 1) % 4, (x + 3) % 4
    yp, ym = (y + 1) % 4, (y + 3) % 4
    f_x = (zh * 16 + xp * 4 + y, zh * 16 + xm * 4 + y)
    f_y = (zh * 16 + x * 4 + yp, zh * 16 + x * 4 + ym)

    def remote(src, dst, ssem, rsem, bb, ff):
        return pltpu.make_async_remote_copy(
            src_ref=src, dst_ref=dst, send_sem=ssem, recv_sem=rsem,
            device_id=(bb, ff), device_id_type=pl.DeviceIdType.MESH)

    barrier = pltpu.get_barrier_semaphore()
    partners = [((b + d) % NB, f) for d in range(1, NB)] + [(b, other)] + [(b, q) for q in f_x + f_y]
    for bb, ff in partners:
        pl.semaphore_signal(barrier, inc=1, device_id=(bb, ff), device_id_type=pl.DeviceIdType.MESH)

    x_copies = [pltpu.make_async_copy(x_hbm.at[pl.ds(r * 256, 256)], xv.at[pl.ds(r * 256, 256)], x_sem.at[r])
                for r in range(NB)]
    own_copy = pltpu.make_async_copy(occ_hbm, occ_all.at[b], own_sem)
    vir_copy = pltpu.make_async_copy(vir_hbm, vir, vir_sem)
    rb_copy = pltpu.make_async_copy(rb_hbm, rb_ref, rb_sem)
    mask_copy = pltpu.make_async_copy(mask_hbm, mask_ref, mask_sem)
    own_copy.start()
    rb_copy.start()
    mask_copy.start()
    for c in x_copies:
        c.start()
    vir_copy.start()

    def occ_copy(d):
        return remote(occ_all.at[b], occ_all.at[b], occ_send.at[d - 1], occ_recv.at[d - 1], (b + d) % NB, f)

    def occ_arrival(d):
        slot = occ_all.at[(b + NB - d) % NB]
        return remote(slot, slot, occ_send.at[d - 1], occ_recv.at[d - 1], (b + d) % NB, f)

    own_copy.wait()
    pl.semaphore_wait(barrier, len(partners))
    for d in range(1, NB):
        occ_copy(d).start()
    rb_copy.wait()
    mask_copy.wait()

    owned = [rb_ref[b * NB + r] for r in range(NB)]
    sub8 = lax.broadcasted_iota(jnp.int32, (NB, 64), 0)
    lane64 = lax.broadcasted_iota(jnp.int32, (NB, 64), 1)
    want = jnp.zeros((NB, 64), jnp.int32)
    for r in range(NB):
        want = jnp.where(sub8 == r, owned[r], want)
    pick = jnp.where(lane64 == want, 1.0, 0.0).astype(BF16)
    rows = jnp.dot(pick, mask_ref[...].astype(F32).astype(BF16), preferred_element_type=F32).astype(BF16)
    spread = jnp.where(
        lax.broadcasted_iota(jnp.int32, (64, N), 1) // BLK == lax.broadcasted_iota(jnp.int32, (64, N), 0),
        1.0, 0.0).astype(BF16)
    mask_cols = jnp.dot(rows, spread, preferred_element_type=F32)
    for r in range(NB):
        x_copies[r].wait()
        m = jnp.broadcast_to(mask_cols[r:r + 1, :], (16, N)).astype(BF16)
        for s in range(16):
            at = pl.ds(r * 256 + s * 16, 16)
            xv[at, :] = xv[at, :] * m

    lane_m = lax.broadcasted_iota(jnp.int32, (128, 128), 1)
    source = jnp.zeros((128, 128), jnp.int32)
    for r in range(NB):
        source = jnp.where(lane_m // BLK == r, owned[r] * BLK + lane_m % BLK, source)
    sub_m = lax.broadcasted_iota(jnp.int32, (128, 128), 0)
    for d in range(1, NB):
        occ_arrival(d).wait_recv()
    occ_sel = jnp.zeros((64, 128), F32)
    for d in range(NB):
        sel = jnp.where(source == sub_m + d * 128, 1.0, 0.0).astype(BF16)
        occ_sel = occ_sel + jnp.dot(occ_all[d], sel, preferred_element_type=F32)
    rep = jnp.where(
        lax.broadcasted_iota(jnp.int32, (128, 2048), 1) // 16 == lax.broadcasted_iota(jnp.int32, (128, 2048), 0),
        1.0, 0.0).astype(BF16)
    t1[...] = jnp.dot(occ_sel.astype(BF16), rep, preferred_element_type=F32)
    vir_copy.wait()

    def sib_copy(c):
        return remote(sib_tx.at[c], sib_rx.at[c], send.at[c, SIB], recv.at[c, SIB], sib, f)

    def z_copy(c, d):
        to = (zl + d) % 4
        return remote(z_tx.at[c, to], z_rx.at[c, d - 1], send.at[c, Z1 + d - 1], recv.at[c, Z1 + d - 1],
                      to * 2 + core, f)

    def zh_copy(c):
        return remote(g.at[0, c, :, ME, ME], g.at[1, c, :, ME, ME], send.at[c, ZH], recv.at[c, ZH], b, other)

    def along_x(k, h):
        return (k + h) % 2 == 0

    def block(k, h, pos, c):
        return g.at[k, c, h, pos, ME] if along_x(k, h) else g.at[k, c, h, ME, pos]

    def group(k, h, lo, n, pos, c):
        if along_x(k, h):
            return g.at[k, c, h, pl.ds(lo, n), pos]
        return g.at[k, c, h, pos, pl.ds(lo, n)]

    def lane_half(ref, h):
        return ref.at[:, pl.ds(h * QUART, QUART)]

    def ring_copy(k, h, j, c, arrival):
        if j in FIRST:
            source, target = FIRST[j]
            src, dst = block(k, h, source, c), block(k, h, target, c)
            if j in (A_FUP, A_FDN):
                src, dst = lane_half(src, j - A_FUP), lane_half(dst, j - A_FUP)
        else:
            source, target, lo, n = SECOND[j]
            src, dst = group(k, h, lo, n, source, c), group(k, h, lo, n, target, c)
        to = f_x if along_x(k, h) == (j in FIRST) else f_y
        dev = to[0] if j in (A_UP, A_FUP, B0_UP, B1_UP, B2_UP, B_FUP) else to[1]
        s = RING + PER_STREAM * (2 * k + h) + j
        return remote(dst if arrival else src, dst, send.at[c, s], recv.at[c, s], b, dev)

    def go(k, j, c, h):
        ring_copy(k, h, j, c, False).start()

    def arrived(k, j, c, h):
        ring_copy(k, h, j, c, True).wait_recv()

    col16 = lax.broadcasted_iota(jnp.int32, (8, 2, 8, 2048), 3) % 16
    row2 = lax.broadcasted_iota(jnp.int32, (8, 2, 8, 2048), 1)

    def stage0(c):
        w = jnp.where(col16 == 2 * c + row2, t1[...].reshape(8, 1, 8, 2048), 0.0)
        w = w.reshape(128, 2048).astype(BF16)
        for h in range(2):
            cols = pl.ds(h * HALF, HALF)
            part = jnp.dot(w, xv[:, cols], preferred_element_type=F32)
            p32[:, :, :, cols] = part.reshape(4, 2, 16, HALF)
        sib_tx[c] = p32[:, 1 - core].astype(BF16)
        sib_copy(c).start()
        zacc[c] = p32[:, core]

    def stage1(c):
        sib_copy(c).wait_recv()
        total = zacc[c] + sib_rx[c].astype(F32)
        zacc[c] = total
        z_tx[c] = total.astype(BF16)
        for d in range(1, 4):
            z_copy(c, d).start()

    def stage2(c):
        half = zacc[c, zl]
        for d in range(1, 4):
            z_copy(c, d).wait_recv()
            half = half + z_rx[c, d - 1].astype(F32)
        for h in range(2):
            g[0, c, h, ME, ME] = half[:, h * HALF:(h + 1) * HALF].astype(BF16)
        zh_copy(c).start()
        for h in range(2):
            go(0, A_UP, c, h)
            go(0, A_DN, c, h)
            go(0, B0_UP, c, h)
            go(0, B0_DN, c, h)

    def stage3(c):
        zh_copy(c).wait_recv()
        for h in range(2):
            go(1, A_UP, c, h)
            go(1, A_DN, c, h)
            go(1, B0_UP, c, h)
            go(1, B0_DN, c, h)

    xo, yo = (x + 2) % 4, (y + 2) % 4
    places = [(k, i, j, plane * 16 + px * 4 + py)
              for k, plane in ((0, zh), (1, 1 - zh))
              for i, px in enumerate((x, xp, xm, xo)) for j, py in enumerate((y, yp, ym, yo))]

    def stage8(c):
        @pl.when(c < NP - 1)
        def _():
            low = g[:, c, 0].reshape(512, HALF)
            high = g[:, c, 1].reshape(512, HALF)
            prod = jnp.dot(low, vir[0:HALF, :], preferred_element_type=F32)
            prod = prod + jnp.dot(high, vir[HALF:N, :], preferred_element_type=F32)
            prod = prod.astype(BF16)
            for n, (_, _, _, at) in enumerate(places):
                done_ref[c, at] = prod[n * 16:(n + 1) * 16]

        @pl.when(c == NP - 1)
        def _():
            for k, i, j, at in places:
                for h in range(2):
                    last_ref[h, at] = g[k, NP - 1, h, i, j]

    def ring(k):
        def forward_first(c):
            for h in range(2):
                arrived(k, A_UP, c, h)
                go(k, A_FUP, c, h)
                arrived(k, A_DN, c, h)
                go(k, A_FDN, c, h)
                go(k, B1_UP, c, h)
                go(k, B1_DN, c, h)

        def turn(c):
            for h in range(2):
                arrived(k, A_FUP, c, h)
                arrived(k, A_FDN, c, h)
                go(k, B2_UP, c, h)
                go(k, B2_DN, c, h)

        def forward_up(c):
            for h in range(2):
                arrived(k, B0_UP, c, h)
                arrived(k, B1_UP, c, h)
                go(k, B_FUP, c, h)

        def forward_down(c):
            for h in range(2):
                arrived(k, B1_DN, c, h)
                arrived(k, B2_DN, c, h)
                go(k, B_FDN, c, h)

        def finish(c):
            for h in range(2):
                for j in (B0_DN, B2_UP, B_FUP, B_FDN):
                    arrived(k, j, c, h)
        return forward_first, turn, forward_up, forward_down, finish

    (a20, a30, a40, a60, a50), (a21, a31, a41, a61, a51) = ring(0), ring(1)
    schedule = ((stage0, 0), (stage1, 0), (stage2, 1), (a20, 2), (a40, 3), (a30, 3), (a60, 4), (stage3, 2), (a21, 3), (a41, 4), (a31, 4), (a61, 5), (a50, 6), (a51, 7), (stage8, 7))

    def step(t, carry):
        for fn, lag in schedule:
            c = t - lag

            @pl.when((c >= 0) & (c < NC))
            def _():
                fn(c)
        return carry

    lax.fori_loop(0, NC + max(lag for _, lag in schedule), step, 0)

    def drain(c, carry):
        sib_copy(c).wait_send()
        for d in range(1, 4):
            z_copy(c, d).wait_send()
        zh_copy(c).wait_send()
        for k in range(2):
            for h in range(2):
                for j in range(PER_STREAM):
                    ring_copy(k, h, j, c, False).wait_send()
        return carry

    lax.fori_loop(0, NC, drain, 0)
    for d in range(1, NB):
        occ_copy(d).wait_send()


def finish_kernel(done_ref, last_ref, vir_ref, out_hbm, tail, sem):
    copies = [pltpu.make_async_copy(done_ref.at[q], out_hbm.at[:, q], sem.at[q]) for q in range(NP - 1)]
    for copy in copies:
        copy.start()
    low, high = last_ref[0].reshape(512, HALF), last_ref[1].reshape(512, HALF)
    prod = jnp.dot(low, vir_ref[0:HALF, :], preferred_element_type=F32)
    prod = prod + jnp.dot(high, vir_ref[HALF:N, :], preferred_element_type=F32)
    tail[...] = prod.astype(BF16).reshape(32, 16, N)
    copy = pltpu.make_async_copy(tail, out_hbm.at[:, NP - 1], sem.at[NP - 1])
    copy.start()
    for copy in copies + [copy]:
        copy.wait()


def shards(integrals, pair_mask, row_blocks, occ_coef, vir_coef):
    x2 = integrals.reshape(2048, N)
    hbm = pl.BlockSpec(memory_space=pl.ANY)
    vmem = pl.BlockSpec(memory_space=pltpu.VMEM)
    done, last, vir = pl.pallas_call(
        kernel,
        out_shape=(pltpu.VMEM((NP - 1, 32, 16, N), BF16), pltpu.VMEM((2, 32, 16, HALF), BF16),
                   pltpu.VMEM((N, N), BF16)),
        in_specs=[pl.BlockSpec(memory_space=pltpu.HBM)] * 5,
        out_specs=(vmem, vmem, vmem),
        scratch_shapes=[
            pltpu.SMEM((NB * NB,), jnp.int32),
            pltpu.VMEM((64, 64), jnp.int32),
            pltpu.VMEM((2048, N), BF16),
            pltpu.VMEM((NB, 64, 128), BF16),
            pltpu.VMEM((64, 2048), F32),
            pltpu.VMEM((4, 2, 16, N), F32),
            pltpu.VMEM((NC, 4, 16, N), F32),
            pltpu.VMEM((NC, 4, 16, N), BF16),
            pltpu.VMEM((NC, 4, 16, N), BF16),
            pltpu.VMEM((NC, 4, 16, N), BF16),
            pltpu.VMEM((NC, 3, 16, N), BF16),
            pltpu.VMEM((2, NP, 2, 4, 4, 16, HALF), BF16),
            pltpu.SemaphoreType.DMA,
            pltpu.SemaphoreType.DMA,
            pltpu.SemaphoreType.DMA((NB,)),
            pltpu.SemaphoreType.DMA,
            pltpu.SemaphoreType.DMA,
            pltpu.SemaphoreType.DMA((NB - 1,)),
            pltpu.SemaphoreType.DMA((NB - 1,)),
            pltpu.SemaphoreType.DMA((NC, KINDS)),
            pltpu.SemaphoreType.DMA((NC, KINDS)),
        ],
        compiler_params=pltpu.CompilerParams(
            collective_id=0, has_side_effects=True, vmem_limit_bytes=53900 * 1024),
        cost_estimate=pl.CostEstimate(flops=13 * 10 ** 9, bytes_accessed=15 * 2 ** 20, transcendentals=0),
    )(row_blocks, pair_mask, x2, occ_coef.T, vir_coef)
    out = pl.pallas_call(
        finish_kernel,
        out_shape=jax.ShapeDtypeStruct((32, NP, 16, N), BF16),
        in_specs=[vmem, vmem, vmem],
        out_specs=hbm,
        scratch_shapes=[pltpu.VMEM((32, 16, N), BF16), pltpu.SemaphoreType.DMA((NP,))],
        compiler_params=pltpu.CompilerParams(vmem_limit_bytes=12 * 2 ** 20),
    )(done, last, vir)
    return out.reshape(512, 8, N)


def solution(mesh):
    placed = (P("basis", "fit", None), P(), P(), P("basis", None), P(None, "fit"))
    return jax.shard_map(
        shards, mesh=mesh, in_specs=placed, out_specs=P(None, "basis", "fit"), check_vma=False
    )
```

```python
import jax
import jax.numpy as jnp
from jax import lax
from jax.experimental import pallas as pl
from jax.experimental.pallas import tpu as pltpu
from jax.sharding import PartitionSpec as P

BLK = 16
NB = 8
NP = 8
NC = 8
N = 1024
HALF = N // 2
QUART = N // 4
F32 = jnp.float32
BF16 = jnp.bfloat16

SIB, Z1, ZH = 0, 2, 8
RING = 10
PER_STREAM = 12
KINDS = RING + 4 * PER_STREAM
A_UP, A_DN, A_FUP, A_FDN, B0_UP, B0_DN, B1_UP, B1_DN, B2_UP, B2_DN, B_FUP, B_FDN = range(PER_STREAM)
ME, UP, DN, OPP = range(4)
FIRST = {A_UP: (ME, DN), A_DN: (ME, UP), A_FUP: (DN, OPP), A_FDN: (UP, OPP)}
SECOND = {B0_UP: (ME, DN, 0, 1), B0_DN: (ME, UP, 0, 1), B1_UP: (ME, DN, 1, 2), B1_DN: (ME, UP, 1, 2),
          B2_UP: (ME, DN, 3, 1), B2_DN: (ME, UP, 3, 1), B_FUP: (DN, OPP, 0, 2), B_FDN: (UP, OPP, 2, 2)}


def kernel(rb_hbm, mask_hbm, x_hbm, occ_hbm, vir_hbm, done_ref, last_ref, vir,
           rb_ref, mask_ref, xv, occ_all, t1, p32, zacc, sib_tx, sib_rx, z_tx, z_rx, g,
           rb_sem, mask_sem, x_sem, vir_sem, own_sem, occ_send, occ_recv, send, recv):
    b = lax.axis_index("basis")
    f = lax.axis_index("fit")
    core, zl = b % 2, b // 2
    zh, x, y = f // 16, (f // 4) % 4, f % 4
    sib = zl * 2 + (1 - core)
    other = (f + 16) % 32
    xp, xm = (x + 1) % 4, (x + 3) % 4
    yp, ym = (y + 1) % 4, (y + 3) % 4
    f_x = (zh * 16 + xp * 4 + y, zh * 16 + xm * 4 + y)
    f_y = (zh * 16 + x * 4 + yp, zh * 16 + x * 4 + ym)

    def remote(src, dst, ssem, rsem, bb, ff):
        return pltpu.make_async_remote_copy(
            src_ref=src, dst_ref=dst, send_sem=ssem, recv_sem=rsem,
            device_id=(bb, ff), device_id_type=pl.DeviceIdType.MESH)

    barrier = pltpu.get_barrier_semaphore()
    partners = [((b + d) % NB, f) for d in range(1, NB)] + [(b, other)] + [(b, q) for q in f_x + f_y]
    for bb, ff in partners:
        pl.semaphore_signal(barrier, inc=1, device_id=(bb, ff), device_id_type=pl.DeviceIdType.MESH)

    x_copies = [pltpu.make_async_copy(x_hbm.at[pl.ds(r * 256, 256)], xv.at[pl.ds(r * 256, 256)], x_sem.at[r])
                for r in range(NB)]
    own_copy = pltpu.make_async_copy(occ_hbm, occ_all.at[b], own_sem)
    vir_copy = pltpu.make_async_copy(vir_hbm, vir, vir_sem)
    rb_copy = pltpu.make_async_copy(rb_hbm, rb_ref, rb_sem)
    mask_copy = pltpu.make_async_copy(mask_hbm, mask_ref, mask_sem)
    own_copy.start()
    rb_copy.start()
    mask_copy.start()
    for c in x_copies:
        c.start()
    vir_copy.start()

    def occ_copy(d):
        return remote(occ_all.at[b], occ_all.at[b], occ_send.at[d - 1], occ_recv.at[d - 1], (b + d) % NB, f)

    def occ_arrival(d):
        slot = occ_all.at[(b + NB - d) % NB]
        return remote(slot, slot, occ_send.at[d - 1], occ_recv.at[d - 1], (b + d) % NB, f)

    own_copy.wait()
    pl.semaphore_wait(barrier, len(partners))
    for d in range(1, NB):
        occ_copy(d).start()
    rb_copy.wait()
    mask_copy.wait()

    owned = [rb_ref[b * NB + r] for r in range(NB)]
    sub8 = lax.broadcasted_iota(jnp.int32, (NB, 64), 0)
    lane64 = lax.broadcasted_iota(jnp.int32, (NB, 64), 1)
    want = jnp.zeros((NB, 64), jnp.int32)
    for r in range(NB):
        want = jnp.where(sub8 == r, owned[r], want)
    pick = jnp.where(lane64 == want, 1.0, 0.0).astype(BF16)
    rows = jnp.dot(pick, mask_ref[...].astype(F32).astype(BF16), preferred_element_type=F32).astype(BF16)
    spread = jnp.where(
        lax.broadcasted_iota(jnp.int32, (64, N), 1) // BLK == lax.broadcasted_iota(jnp.int32, (64, N), 0),
        1.0, 0.0).astype(BF16)
    mask_cols = jnp.dot(rows, spread, preferred_element_type=F32)
    for r in range(NB):
        x_copies[r].wait()
        m = jnp.broadcast_to(mask_cols[r:r + 1, :], (16, N)).astype(BF16)
        for s in range(16):
            at = pl.ds(r * 256 + s * 16, 16)
            xv[at, :] = xv[at, :] * m

    lane_m = lax.broadcasted_iota(jnp.int32, (128, 128), 1)
    source = jnp.zeros((128, 128), jnp.int32)
    for r in range(NB):
        source = jnp.where(lane_m // BLK == r, owned[r] * BLK + lane_m % BLK, source)
    sub_m = lax.broadcasted_iota(jnp.int32, (128, 128), 0)
    for d in range(1, NB):
        occ_arrival(d).wait_recv()
    occ_sel = jnp.zeros((64, 128), F32)
    for d in range(NB):
        sel = jnp.where(source == sub_m + d * 128, 1.0, 0.0).astype(BF16)
        occ_sel = occ_sel + jnp.dot(occ_all[d], sel, preferred_element_type=F32)
    rep = jnp.where(
        lax.broadcasted_iota(jnp.int32, (128, 2048), 1) // 16 == lax.broadcasted_iota(jnp.int32, (128, 2048), 0),
        1.0, 0.0).astype(BF16)
    t1[...] = jnp.dot(occ_sel.astype(BF16), rep, preferred_element_type=F32)

    def sib_copy(c, h):
        return remote(sib_tx.at[c, h], sib_rx.at[c, h], send.at[c, SIB + h], recv.at[c, SIB + h], sib, f)

    def z_copy(c, d, h):
        to = (zl + d) % 4
        s = Z1 + 3 * h + d - 1
        return remote(z_tx.at[c, h, to], z_rx.at[c, h, d - 1], send.at[c, s], recv.at[c, s], to * 2 + core, f)

    def zh_copy(c, h):
        return remote(g.at[0, c, h, ME, ME], g.at[1, c, h, ME, ME], send.at[c, ZH + h], recv.at[c, ZH + h], b, other)

    def along_x(k, h):
        return (k + h) % 2 == 0

    def block(k, h, pos, c):
        return g.at[k, c, h, pos, ME] if along_x(k, h) else g.at[k, c, h, ME, pos]

    def group(k, h, lo, n, pos, c):
        if along_x(k, h):
            return g.at[k, c, h, pl.ds(lo, n), pos]
        return g.at[k, c, h, pos, pl.ds(lo, n)]

    def lane_half(ref, h):
        return ref.at[:, pl.ds(h * QUART, QUART)]

    def ring_copy(k, h, j, c, arrival):
        if j in FIRST:
            source, target = FIRST[j]
            src, dst = block(k, h, source, c), block(k, h, target, c)
            if j in (A_FUP, A_FDN):
                src, dst = lane_half(src, j - A_FUP), lane_half(dst, j - A_FUP)
        else:
            source, target, lo, n = SECOND[j]
            src, dst = group(k, h, lo, n, source, c), group(k, h, lo, n, target, c)
        to = f_x if along_x(k, h) == (j in FIRST) else f_y
        dev = to[0] if j in (A_UP, A_FUP, B0_UP, B1_UP, B2_UP, B_FUP) else to[1]
        s = RING + PER_STREAM * (2 * k + h) + j
        return remote(dst if arrival else src, dst, send.at[c, s], recv.at[c, s], b, dev)

    def go(k, j, c, h):
        ring_copy(k, h, j, c, False).start()

    def arrived(k, j, c, h):
        ring_copy(k, h, j, c, True).wait_recv()

    col16 = lax.broadcasted_iota(jnp.int32, (8, 2, 8, 2048), 3) % 16
    row2 = lax.broadcasted_iota(jnp.int32, (8, 2, 8, 2048), 1)

    def stage0(c):
        w = jnp.where(col16 == 2 * c + row2, t1[...].reshape(8, 1, 8, 2048), 0.0)
        w = w.reshape(128, 2048).astype(BF16)
        for h in range(2):
            cols = pl.ds(h * HALF, HALF)
            part = jnp.dot(w, xv[:, cols], preferred_element_type=F32)
            p32[h] = part.reshape(4, 2, 16, HALF)
            sib_tx[c, h] = p32[h, :, 1 - core].astype(BF16)
            sib_copy(c, h).start()

    def stage1(c):
        for h in range(2):
            sib_copy(c, h).wait_recv()
            total = p32[h, :, core] + sib_rx[c, h].astype(F32)
            zacc[c, h] = total
            z_tx[c, h] = total.astype(BF16)
            for d in range(1, 4):
                z_copy(c, d, h).start()

    def stage2(c):
        for h in range(2):
            half = zacc[c, h, zl]
            for d in range(1, 4):
                z_copy(c, d, h).wait_recv()
                half = half + z_rx[c, h, d - 1].astype(F32)
            g[0, c, h, ME, ME] = half.astype(BF16)
            zh_copy(c, h).start()
            go(0, A_UP, c, h)
            go(0, A_DN, c, h)
            go(0, B0_UP, c, h)
            go(0, B0_DN, c, h)

    def stage3(c):
        for h in range(2):
            zh_copy(c, h).wait_recv()
            go(1, A_UP, c, h)
            go(1, A_DN, c, h)
            go(1, B0_UP, c, h)
            go(1, B0_DN, c, h)

    xo, yo = (x + 2) % 4, (y + 2) % 4
    places = [(k, i, j, plane * 16 + px * 4 + py)
              for k, plane in ((0, zh), (1, 1 - zh))
              for i, px in enumerate((x, xp, xm, xo)) for j, py in enumerate((y, yp, ym, yo))]

    def stage8(c):
        @pl.when(c < NP - 1)
        def _():
            low = g[:, c, 0].reshape(512, HALF)
            high = g[:, c, 1].reshape(512, HALF)
            prod = jnp.dot(low, vir[0:HALF, :], preferred_element_type=F32)
            prod = prod + jnp.dot(high, vir[HALF:N, :], preferred_element_type=F32)
            prod = prod.astype(BF16)
            for n, (_, _, _, at) in enumerate(places):
                done_ref[c, at] = prod[n * 16:(n + 1) * 16]

        @pl.when(c == NP - 1)
        def _():
            for k, i, j, at in places:
                for h in range(2):
                    last_ref[h, at] = g[k, NP - 1, h, i, j]

    def ring(k):
        def forward_first(c):
            for h in range(2):
                arrived(k, A_UP, c, h)
                go(k, A_FUP, c, h)
                arrived(k, A_DN, c, h)
                go(k, A_FDN, c, h)
                go(k, B1_UP, c, h)
                go(k, B1_DN, c, h)

        def turn(c):
            for h in range(2):
                arrived(k, A_FUP, c, h)
                arrived(k, A_FDN, c, h)
                go(k, B2_UP, c, h)
                go(k, B2_DN, c, h)

        def forward_up(c):
            for h in range(2):
                arrived(k, B0_UP, c, h)
                arrived(k, B1_UP, c, h)
                go(k, B_FUP, c, h)

        def forward_down(c):
            for h in range(2):
                arrived(k, B1_DN, c, h)
                arrived(k, B2_DN, c, h)
                go(k, B_FDN, c, h)

        def finish(c):
            for h in range(2):
                for j in (B0_DN, B2_UP, B_FUP, B_FDN):
                    arrived(k, j, c, h)
        return forward_first, turn, forward_up, forward_down, finish

    (a20, a30, a40, a60, a50), (a21, a31, a41, a61, a51) = ring(0), ring(1)
    schedule = ((stage0, 0), (stage1, 0), (stage2, 1), (a20, 2), (a40, 3), (a30, 3), (a60, 4), (stage3, 2), (a21, 3), (a41, 4), (a31, 4), (a61, 5), (a50, 6), (a51, 7), (stage8, 7))

    def step(t, carry):
        @pl.when(t == 3)
        def _():
            vir_copy.wait()

        for fn, lag in schedule:
            c = t - lag

            @pl.when((c >= 0) & (c < NC))
            def _():
                fn(c)
        return carry

    lax.fori_loop(0, NC + max(lag for _, lag in schedule), step, 0)

    def drain(c, carry):
        for h in range(2):
            sib_copy(c, h).wait_send()
            for d in range(1, 4):
                z_copy(c, d, h).wait_send()
            zh_copy(c, h).wait_send()
        for k in range(2):
            for h in range(2):
                for j in range(PER_STREAM):
                    ring_copy(k, h, j, c, False).wait_send()
        return carry

    lax.fori_loop(0, NC, drain, 0)
    for d in range(1, NB):
        occ_copy(d).wait_send()


def finish_kernel(done_ref, last_ref, vir_ref, out_hbm, tail, sem):
    copies = [pltpu.make_async_copy(done_ref.at[q], out_hbm.at[:, q], sem.at[q]) for q in range(NP - 1)]
    for copy in copies:
        copy.start()
    low, high = last_ref[0].reshape(512, HALF), last_ref[1].reshape(512, HALF)
    prod = jnp.dot(low, vir_ref[0:HALF, :], preferred_element_type=F32)
    prod = prod + jnp.dot(high, vir_ref[HALF:N, :], preferred_element_type=F32)
    tail[...] = prod.astype(BF16).reshape(32, 16, N)
    copy = pltpu.make_async_copy(tail, out_hbm.at[:, NP - 1], sem.at[NP - 1])
    copy.start()
    for copy in copies + [copy]:
        copy.wait()


def shards(integrals, pair_mask, row_blocks, occ_coef, vir_coef):
    x2 = integrals.reshape(2048, N)
    hbm = pl.BlockSpec(memory_space=pl.ANY)
    vmem = pl.BlockSpec(memory_space=pltpu.VMEM)
    done, last, vir = pl.pallas_call(
        kernel,
        out_shape=(pltpu.VMEM((NP - 1, 32, 16, N), BF16), pltpu.VMEM((2, 32, 16, HALF), BF16),
                   pltpu.VMEM((N, N), BF16)),
        in_specs=[pl.BlockSpec(memory_space=pltpu.HBM)] * 5,
        out_specs=(vmem, vmem, vmem),
        scratch_shapes=[
            pltpu.SMEM((NB * NB,), jnp.int32),
            pltpu.VMEM((64, 64), jnp.int32),
            pltpu.VMEM((2048, N), BF16),
            pltpu.VMEM((NB, 64, 128), BF16),
            pltpu.VMEM((64, 2048), F32),
            pltpu.VMEM((2, 4, 2, 16, HALF), F32),
            pltpu.VMEM((NC, 2, 4, 16, HALF), F32),
            pltpu.VMEM((NC, 2, 4, 16, HALF), BF16),
            pltpu.VMEM((NC, 2, 4, 16, HALF), BF16),
            pltpu.VMEM((NC, 2, 4, 16, HALF), BF16),
            pltpu.VMEM((NC, 2, 3, 16, HALF), BF16),
            pltpu.VMEM((2, NP, 2, 4, 4, 16, HALF), BF16),
            pltpu.SemaphoreType.DMA,
            pltpu.SemaphoreType.DMA,
            pltpu.SemaphoreType.DMA((NB,)),
            pltpu.SemaphoreType.DMA,
            pltpu.SemaphoreType.DMA,
            pltpu.SemaphoreType.DMA((NB - 1,)),
            pltpu.SemaphoreType.DMA((NB - 1,)),
            pltpu.SemaphoreType.DMA((NC, KINDS)),
            pltpu.SemaphoreType.DMA((NC, KINDS)),
        ],
        compiler_params=pltpu.CompilerParams(
            collective_id=0, has_side_effects=True, vmem_limit_bytes=53900 * 1024),
        cost_estimate=pl.CostEstimate(flops=13 * 10 ** 9, bytes_accessed=15 * 2 ** 20, transcendentals=0),
    )(row_blocks, pair_mask, x2, occ_coef.T, vir_coef)
    out = pl.pallas_call(
        finish_kernel,
        out_shape=jax.ShapeDtypeStruct((32, NP, 16, N), BF16),
        in_specs=[vmem, vmem, vmem],
        out_specs=hbm,
        scratch_shapes=[pltpu.VMEM((32, 16, N), BF16), pltpu.SemaphoreType.DMA((NP,))],
        compiler_params=pltpu.CompilerParams(vmem_limit_bytes=12 * 2 ** 20),
    )(done, last, vir)
    return out.reshape(512, 8, N)


def solution(mesh):
    placed = (P("basis", "fit", None), P(), P(), P("basis", None), P(None, "fit"))
    return jax.shard_map(
        shards, mesh=mesh, in_specs=placed, out_specs=P(None, "basis", "fit"), check_vma=False
    )
```
